32 devices in a mesh: mock: 4 (over y, core), row: 8 (over z, x).
Axes of the slice: x: 2, y: 2, z: 4, core: 2. Of those that a mesh axis runs over, the one named last changes fastest.
Arguments:
- mock_maps: float32 [128, 4, 4096], P('mock', None, 'row'), parts along dimension 0, may hold values from -6 to 6
- pixel_order: int32 [4, 4096], P(None, 'row'), may hold values from 0 to 4095, as said below
- prior_solution: bfloat16 [128, 4096], P('mock', 'row'), parts along dimension 0, may hold values from -6 to 6
- factor_rows: bfloat16 [4, 4096, 3, 256], P(None, 'row'), may hold values from -0.109375 to 0.109375
- tile_columns: int32 [4, 16, 3], replicated, may hold values from 0 to 63, as said below
- panel_inverse: bfloat16 [4, 4096, 4096], P(None, 'row'), as said below
Outputs:
- whitened: float32 [128, 4, 4096], P('mock', None, 'row'), parts along dimension 0
The draws below stay inside these ranges and needn't reach their ends.
There are 4 independent parts, one for each index of `mock`. The reference program is written for one: setup_inputs(seed, part) draws one part's arguments, and reference() takes and returns one part's arrays. A program takes and returns all parts, laid end to end along the dimension named above; an argument that names none is the same for every part. Nothing has to cross between parts.
Inputs may be any that keep to these rules, and one draw needn't show every extreme that they name: `pixel_order`: each aligned block of 512 entries of a panel is a permutation of its own indices within the panel. `tile_columns`: slot 0 of tile row j of panel p is p * 16 + j, slot 1 is p * 16 + ((j + 8) mod 16), and slot 2 is below (p + 1) * 16: tiles lie only in columns solved before the row's panel. `panel_inverse`: within each panel the matrix is lower triangular with a positive diagonal.
All inputs are finite; a program needn't handle non-finite values.
Results may differ from the reference program's by a relative error of at most 0.0036.
Values may be sent and summed in bfloat16 or wider, within the bound.
A program may use at most 128 MiB of HBM per device.

```python
import math
import jax
import jax.numpy as jnp

MOCKS = 32
TILE = 256
PANEL = 4096
PANELS = 4
SLOTS = 3
PRIOR = 4096
PER_PANEL = 16
SHARE = 512


def draw_pixel_order(key, part):
    block_count = PANELS * (PANEL // SHARE)
    block_keys = jax.random.split(key, block_count)
    local_order = jax.vmap(lambda single: jax.random.permutation(single, SHARE))(block_keys)
    offsets = (jnp.arange(block_count, dtype=jnp.int32) % (PANEL // SHARE) * SHARE)[:, None]
    return (local_order.astype(jnp.int32) + offsets).reshape(PANELS, PANEL)


def draw_tile_columns(key, part):
    panel_index = jnp.arange(PANELS, dtype=jnp.int32)[:, None]
    tile_index = jnp.arange(PER_PANEL, dtype=jnp.int32)[None, :]
    base = panel_index * PER_PANEL
    same_place = base + tile_index
    opposite = base + (tile_index + PER_PANEL // 2) % PER_PANEL
    limits = jnp.broadcast_to(base + PER_PANEL, (PANELS, PER_PANEL))
    random_cols = jax.random.randint(key, (PANELS, PER_PANEL), 0, limits, dtype=jnp.int32)
    return jnp.stack([same_place, opposite, random_cols], axis=2).astype(jnp.int32)


def draw_panel_inverse(key, part):
    first_key, second_key = jax.random.split(key)
    local_row = jnp.arange(PANEL, dtype=jnp.int32)[None, :, None]
    column = jnp.arange(PANEL, dtype=jnp.int32)[None, None, :]
    noise = jax.random.normal(first_key, (PANELS, PANEL, PANEL), jnp.float32) * (0.5 / math.sqrt(PANEL))
    diagonal = jax.random.uniform(second_key, (PANELS, PANEL, 1), jnp.float32, 0.6, 1.4)
    lower = jnp.where(column < local_row, noise, 0.0)
    return (lower + jnp.where(column == local_row, diagonal, 0.0)).astype(jnp.bfloat16)


def shard_levels(rng, shape, cuts, least, top_value):
    level, own = 1.0, jax.random.fold_in(rng, 6)
    for axis_at, shards_of in cuts:
        steps = jnp.exp(jax.random.uniform(jax.random.fold_in(own, axis_at), (shards_of,), jnp.float32, least / len(cuts), top_value / len(cuts)))
        level = level * jnp.repeat(steps, shape[axis_at] // shards_of).reshape([-1 if axis == axis_at else 1 for axis in range(len(shape))])
    return level


def bell_draw(key, shape, deviation, limit, cuts=(), kind=jnp.bfloat16):
    factor_of = shard_levels(key, shape, cuts, -0.22, 0.18) if cuts else 1.0
    result = jax.random.normal(key, shape, jnp.float32) * deviation * factor_of
    return jnp.minimum(jnp.maximum(result, -limit), limit).astype(kind)


def setup_inputs(seed: int = 0, part: int = 0) -> dict:
    seeds = jax.random.split(jax.random.key(seed), 7)
    part_splits = jax.random.split(jax.random.fold_in(seeds[6], part), 7)
    mock_maps = bell_draw(part_splits[0], (MOCKS, PANELS, PANEL), 1.0, 6.0, ((2, 8),), jnp.float32)
    pixel_order = draw_pixel_order(jax.random.fold_in(seeds[6], 71), part)
    prior_solution = bell_draw(part_splits[2], (MOCKS, PRIOR), 1.0, 6.0, ((1, 8),))
    factor_rows = bell_draw(seeds[3], (PANELS, PANEL, SLOTS, TILE), (4 * SLOTS * TILE) ** -0.5, 0.109375, ((1, 8),))
    tile_columns = draw_tile_columns(jax.random.fold_in(seeds[6], 71), part)
    panel_inverse = draw_panel_inverse(jax.random.fold_in(seeds[6], 71), part)
    return {"mock_maps": mock_maps, "pixel_order": pixel_order, "prior_solution": prior_solution, "factor_rows": factor_rows, "tile_columns": tile_columns, "panel_inverse": panel_inverse}


def reference(mock_maps, pixel_order, prior_solution, factor_rows, tile_columns, panel_inverse):
    index_table = jnp.broadcast_to(pixel_order[None], mock_maps.shape)
    ordered = jnp.take_along_axis(mock_maps, index_table, axis=2)
    mock_count = mock_maps.shape[0]
    known_rows = jnp.concatenate([prior_solution, jnp.zeros((mock_count, PANELS * PANEL), prior_solution.dtype)], axis=1)
    pieces = []
    for panel_step in range(PANELS):
        tile_view = known_rows.reshape(mock_count, -1, TILE)
        picked = jnp.take(tile_view, tile_columns[panel_step], axis=1).astype(jnp.float32)
        factor_tiles = factor_rows[panel_step].reshape(PER_PANEL, TILE, SLOTS, TILE).astype(jnp.float32)
        update = jnp.einsum("mtkc,tskc->mts", picked, factor_tiles).reshape(mock_count, PANEL)
        residual = (ordered[:, panel_step] - update).astype(jnp.bfloat16)
        solved = jnp.dot(residual, panel_inverse[panel_step].T, preferred_element_type=jnp.float32)
        pieces.append(solved)
        begin = PRIOR + panel_step * PANEL
        known_rows = known_rows.at[:, begin:begin + PANEL].set(solved.astype(known_rows.dtype))
    return jnp.stack(pieces, axis=1)
```

```python
import functools

import jax
import jax.numpy as jnp
from jax import lax
from jax.experimental import pallas as pl
from jax.experimental.pallas import tpu as pltpu
from jax.sharding import PartitionSpec as P

MESH = pl.DeviceIdType.MESH
NT = (((1,), (1,)), ((), ()))
GROUPS = 2


def solve_kernel(
    n, tile, columns_ref, order_hbm, maps_hbm, prior_hbm, factor_hbm, inverse_hbm, out_hbm,
    order_ref, maps_ref, out_ref, map_sem, out_sem, residuals, inverse, factor, ordered, total,
    local_sem, factor_sem, inverse_sem, known_send, known_recv, res_send, res_recv, *blocks,
):
    me = lax.axis_index("row")
    panels, groups, part, share = out_ref.shape
    mocks = groups * part
    knowns = [blocks[p * groups : (p + 1) * groups] for p in range(panels)]
    width = blocks[0].shape[2]
    per_tile = tile // width
    pieces = share // width
    prior_pieces = prior_hbm.shape[1] // width
    rows_of = min(share, tile)

    if n & (n - 1) == 0:
        peers = [me ^ d for d in [*range(n - 1, 0, -2), *range(n - 2, 0, -2)]]
    else:
        peers = [lax.rem(me + d, n) for d in range(1, n)]

    barrier = pltpu.get_barrier_semaphore()

    @pl.loop(1, n)
    def _(d):
        pl.semaphore_signal(
            barrier, inc=1, device_id={"row": lax.rem(me + d, n)}, device_id_type=MESH
        )

    def mocks_of(g):
        return pl.ds(g * part, part)

    prior_copies = []
    for g in range(groups):
        for h in range(prior_pieces):
            prior_copies.append(
                pltpu.make_async_copy(
                    prior_hbm.at[mocks_of(g), pl.ds(h * width, width)],
                    knowns[0][g].at[me * prior_pieces + h],
                    local_sem.at[g, h],
                )
            )
    factor_copies, inverse_copies = [], []
    for p in range(panels):
        factor_copies.append(
            pltpu.make_async_copy(factor_hbm.at[p], factor.at[p], factor_sem.at[p])
        )
        inverse_copies.append(
            pltpu.make_async_copy(inverse_hbm.at[p], inverse.at[p], inverse_sem.at[p])
        )
    for c in prior_copies:
        c.start()
    map_copies = [
        pltpu.make_async_copy(order_hbm, order_ref, map_sem.at[0]),
        pltpu.make_async_copy(maps_hbm, maps_ref, map_sem.at[1]),
    ]
    for c in map_copies:
        c.start()
    for p in range(panels):
        factor_copies[p].start()
        inverse_copies[p].start()

    def send_known(p, g):
        count = knowns[p][g].shape[0] // n
        block = knowns[p][g].at[pl.ds(me * count, count)]
        for peer in peers:
            pltpu.make_async_remote_copy(
                src_ref=block,
                dst_ref=block,
                send_sem=known_send.at[p, g],
                recv_sem=known_recv.at[p, g],
                device_id={"row": peer},
                device_id_type=MESH,
            ).start()

    def wait_known(sem, p, g):
        count = knowns[p][g].shape[0] // n
        whole = knowns[p][g].at[pl.ds(0, (n - 1) * count)]
        pltpu.make_async_copy(whole, whole, sem.at[p, g]).wait()

    def residual_copy(p, g, src, dst):
        return pltpu.make_async_remote_copy(
            src_ref=residuals.at[p, g, src],
            dst_ref=residuals.at[p, g, src],
            send_sem=res_send.at[p, g, dst],
            recv_sem=res_recv.at[p, g, src],
            device_id={"row": dst},
            device_id_type=MESH,
        )

    for c in prior_copies:
        c.wait()
    pl.semaphore_wait(barrier, n - 1)
    for g in range(groups):
        send_known(0, g)

    for c in map_copies:
        c.wait()
    places = lax.broadcasted_iota(jnp.int32, (share, share), 0) + me * share

    def gather(p):
        chosen = jnp.where(places == order_ref[pl.ds(p, 1), :], 1.0, 0.0).astype(jnp.bfloat16)
        values = maps_ref[:, p, :]
        high = values.astype(jnp.bfloat16)
        rest = values - high.astype(jnp.float32)
        middle = rest.astype(jnp.bfloat16)
        low = (rest - middle.astype(jnp.float32)).astype(jnp.bfloat16)
        parts = jnp.concatenate([high, middle, low], axis=0)
        taken = jnp.dot(parts, chosen, preferred_element_type=jnp.float32)
        ordered[p] = (taken[:mocks] + taken[mocks : 2 * mocks]) + taken[2 * mocks :]

    gather(0)

    def known_tile(q, g, at):
        return [knowns[q][g][at * per_tile + h] for h in range(per_tile)]

    def picked(p, g, column):
        chosen, low = None, 0
        for q in range(p + 1):
            tiles = knowns[q][g].shape[0] // per_tile
            found = known_tile(q, g, jnp.clip(column - low, 0, tiles - 1))
            if chosen is None:
                chosen = found
            else:
                chosen = [jnp.where(column >= low, new, old) for new, old in zip(found, chosen)]
            low += tiles
        return chosen

    panel_tiles = n * share // tile
    first_tile = me * share // tile
    row_groups = range(share // rows_of)

    def slot_update(p, j, k, parts):
        update = jnp.zeros((part, rows_of), jnp.float32)
        for h in range(per_tile):
            update += lax.dot_general(
                parts[h],
                factor[p, k, j * rows_of : (j + 1) * rows_of, h * width : (h + 1) * width],
                NT,
                preferred_element_type=jnp.float32,
            )
        return update

    def residual_phase(p, g):
        early = None
        if share >= tile:
            early = [slot_update(p, j, 0, known_tile(p, g, first_tile + j)) for j in row_groups]

        wait_known(known_recv, p, g)
        for j in row_groups:
            row_tile = first_tile + j
            update = early[j] if early else slot_update(p, j, 0, known_tile(p, g, row_tile))
            opposite = lax.rem(row_tile + panel_tiles // 2, panel_tiles)
            update += slot_update(p, j, 1, known_tile(p, g, opposite))
            for k in range(2, factor.shape[1]):
                update += slot_update(p, j, k, picked(p, g, columns_ref[k, p, row_tile]))
            span = slice(j * rows_of, (j + 1) * rows_of)
            held = ordered[p, g * part : (g + 1) * part, span]
            residuals[p, g, me, :, span] = (held - update).astype(jnp.bfloat16)

        @pl.loop(0, n - 1 - me)
        def _(k):
            residual_copy(p, g, me, n - 1 - k).start()

    def product_phase(p, g):
        def product(src):
            return lax.dot_general(
                residuals[p, g, src],
                inverse[p, :, pl.ds(pl.multiple_of(src * share, share), share)],
                NT,
                preferred_element_type=jnp.float32,
            )

        total[...] = product(me)

        @pl.loop(1, me + 1)
        def _(d):
            src = me - d
            residual_copy(p, g, src, me).wait_recv()
            total[...] += product(src)

        solved = total[...]
        if p < panels - 1:
            for h in range(pieces):
                knowns[p + 1][g][me * pieces + h] = solved[:, h * width : (h + 1) * width].astype(
                    jnp.bfloat16
                )
            send_known(p + 1, g)
        out_ref[p, g] = solved
        pltpu.make_async_copy(
            out_ref.at[p, g], out_hbm.at[p, mocks_of(g)], out_sem.at[p, g]
        ).start()

    for p in range(panels):
        factor_copies[p].wait()
        for g in range(groups):
            residual_phase(p, g)
        if p + 1 < panels:
            gather(p + 1)
        inverse_copies[p].wait()
        for g in range(groups):
            product_phase(p, g)

    for p in range(panels):
        for g in range(groups):
            wait_known(known_send, p, g)
            pltpu.make_async_copy(
                out_ref.at[p, g], out_hbm.at[p, mocks_of(g)], out_sem.at[p, g]
            ).wait()

            @pl.loop(0, n - 1 - me)
            def _(k):
                residual_copy(p, g, me, n - 1 - k).wait_send()


def per_device(n, mock_maps, pixel_order, prior_solution, factor_rows, tile_columns, panel_inverse):
    mocks, panels, share = mock_maps.shape
    slots, tile = factor_rows.shape[2:]
    width = min(share, tile, prior_solution.shape[1])
    prior_pieces = prior_solution.shape[1] // width
    groups = GROUPS
    part = mocks // groups
    factor_slots = jnp.transpose(factor_rows, (0, 2, 1, 3))
    columns = jnp.transpose(tile_columns, (2, 0, 1))
    known_pieces = [n * prior_pieces] + [n * share // width] * (panels - 1)
    any_spec = pl.BlockSpec(memory_space=pl.ANY)
    dma = pltpu.SemaphoreType.DMA
    out = pl.pallas_call(
        functools.partial(solve_kernel, n, tile),
        out_shape=jax.ShapeDtypeStruct((panels, mocks, share), jnp.float32),
        in_specs=[
            pl.BlockSpec(memory_space=pltpu.SMEM), any_spec, any_spec,
            any_spec, any_spec, any_spec,
        ],
        out_specs=any_spec,
        scratch_shapes=[
            pltpu.VMEM(pixel_order.shape, jnp.int32),
            pltpu.VMEM(mock_maps.shape, jnp.float32),
            pltpu.VMEM((panels, groups, part, share), jnp.float32),
            dma((2,)),
            dma((panels, groups)),
            pltpu.VMEM((panels, groups, n, part, share), jnp.bfloat16),
            pltpu.VMEM(panel_inverse.shape, jnp.bfloat16),
            pltpu.VMEM(factor_slots.shape, jnp.bfloat16),
            pltpu.VMEM((panels, mocks, share), jnp.float32),
            pltpu.VMEM((part, share), jnp.float32),
            dma((groups, prior_pieces)),
            dma((panels,)),
            dma((panels,)),
            dma((panels, groups)),
            dma((panels, groups)),
            dma((panels, groups, n)),
            dma((panels, groups, n)),
        ]
        + [
            pltpu.VMEM((count, part, width), jnp.bfloat16)
            for count in known_pieces
            for _ in range(groups)
        ],
        compiler_params=pltpu.CompilerParams(
            collective_id=0, has_side_effects=True, vmem_limit_bytes=60 * 1024 * 1024
        ),
    )(columns, pixel_order, mock_maps, prior_solution, factor_slots, panel_inverse)
    return jnp.transpose(out, (1, 0, 2))


def solution(mesh):
    return jax.shard_map(
        functools.partial(per_device, mesh.shape["row"]),
        mesh=mesh,
        in_specs=(
            P("mock", None, "row"),
            P(None, "row"),
            P("mock", "row"),
            P(None, "row", None, None),
            P(),
            P(None, "row", None),
        ),
        out_specs=P("mock", None, "row"),
        check_vma=False,
    )
```
